32 devices in a mesh: groups: 2 (over x), tile: 16 (over z, y, core).
Axes of the slice: x: 2, y: 2, z: 4, core: 2. Of those that a mesh axis runs over, the one named last changes fastest.
Arguments:
- image: float32 [4, 768, 4096], P(None, ('groups', 'tile')), parts along dimension 1, may hold values from -6 to 6
- inv_var: float32 [4, 768, 4096], P(None, ('groups', 'tile')), parts along dimension 1, may hold values from 0.25 to 4
- shift: float32 [8, 2], P('groups'), parts along dimension 0, may hold values from -0.5 to 0.5
- col_offset: int32 [8], P('groups'), parts along dimension 0, may hold values from -8 to 8
- psf_rows: float32 [8, 3, 41], P('groups'), parts along dimension 0, may hold values from -1 to 1
- psf_cols: float32 [8, 3, 41], P('groups'), parts along dimension 0, may hold values from -0.5 to 0.5
- placement: int32 [4096, 1], P(('groups', 'tile')), parts along dimension 0, may hold values from 0 to 15; in each aligned block of 128 rows (0 to 127, 128 to 255, ...) at most 16 rows name the same one
Outputs:
- matched: bfloat16 [4, 768, 4096], P(None, ('groups', 'tile')), parts along dimension 1
- coadd: float32 [32, 24, 128], P(('groups', 'tile')), parts along dimension 0
The draws below stay inside these ranges and needn't reach their ends.
There are 2 independent parts, one for each index of `groups`. The reference program is written for one: setup_inputs(seed, part) draws one part's arguments, and reference() takes and returns one part's arrays. A program takes and returns all parts, laid end to end along the dimension named above; each array names one. Nothing has to cross between parts.
Inputs may be any that keep to these rules, and one draw needn't show every extreme that they name: `placement`: every patch receives at least one piece; within the pieces of one device no patch is named more than 16 times, a bound that some block reaches.
All inputs are finite; a program needn't handle non-finite values.
Results may differ from the reference program's by a relative error of at most 0.001.
Values sent between devices are 32-bit elements; how exact they have to be, the bound alone decides.
No kernel may reach another device: no remote copies, remote signals or barrier semaphores. Data moves between devices by JAX's collectives and lax.ppermute only.
A program may use at most 192 MiB of HBM per device.

```python
import math
import jax
import jax.numpy as jnp
import numpy as np
from jax import lax

RD = 24
V = 4
W = 4096
K = 3
PC = 128
ROWS = 384
PIECES = 2048
CAP = 16
N_TILE = 16


def touch_ends(values, own_key, smallest, largest):
    shape = values.shape
    spot = [jax.random.randint(jax.random.fold_in(own_key, axis), (), 0, shape[axis]) for axis in range(len(shape))]
    values = values.at[tuple(spot)].set(smallest)
    longest = shape.index(max(shape))
    spot[longest] = (spot[longest] + 1) % shape[longest]
    return values.at[tuple(spot)].set(largest)


def shard_levels(own_key, dims, cuts, low, largest):
    def one(axis_at, shards_of):
        heights = jax.random.uniform(jax.random.fold_in(jax.random.fold_in(own_key, 6), axis_at), (shards_of,), jnp.float32, low / len(cuts), largest / len(cuts))
        return jnp.repeat(jnp.exp(heights), dims[axis_at] // shards_of).reshape((-1,) + (1,) * (len(dims) - axis_at - 1))

    gain = one(*cuts[0])
    for cut in cuts[1:]:
        gain = gain * one(*cut)
    return gain


def routed_block(stream_key, own, number, rows, count, top, bound, slope):
    ranking = jax.random.permutation(stream_key, count)
    packed, common = portions_of(count, rows * top, bound, slope, True), portions_of(count, rows * top, bound, slope, False)
    places = jnp.arange(count)

    def named(sizes, turn):
        used = int((sizes > 0).sum())
        fixed = max(1, used // 4)
        moved = fixed + (places - fixed + turn * (used - fixed)) % max(1, count - fixed)
        return jnp.zeros((count,), jnp.int32).at[ranking[jnp.where(places < fixed, places, moved)]].set(jnp.asarray(sizes, jnp.int32))

    sizes = jnp.where(number % 4 == 0, named(packed, number // 4), named(common, number - number // 4 - 1))
    mixed = jax.random.permutation(jax.random.fold_in(own, 3), count)
    source_of, sink = mixed[0:count // 2 * 2:2], mixed[1:count // 2 * 2:2]
    margin = jnp.minimum(sizes[source_of] - 1, bound - sizes[sink]) // 2
    margin = jnp.where((source_of == ranking[0]) | (sink == ranking[0]) | (sizes[sink] == 0), 0, jnp.maximum(margin, 0))
    moved = jax.random.randint(jax.random.fold_in(own, 4), (count // 2,), 0, 1 << 20) % (margin + 1)
    sizes = sizes.at[source_of].add(-moved).at[sink].add(moved)
    members = jnp.searchsorted(jnp.cumsum(sizes), jnp.arange(rows * top), side="right").astype(jnp.int32)
    grid = members.reshape(top, rows).T
    grid = grid[jax.random.permutation(jax.random.fold_in(own, 1), rows)]
    turn = jax.random.randint(jax.random.fold_in(own, 2), (rows, 1), 0, top)
    return jnp.take_along_axis(grid, (jnp.arange(top)[None, :] + turn) % top, axis=1)


def portions_of(amount, total, reach, slope, full):
    weights = [(1 << 20) // math.isqrt(rank ** slope) + 1 for rank in range(1, amount + 1)]
    largest = reach if full else min(reach, max(-(-total // amount), total * weights[0] // sum(weights)))
    least = 1 if total - largest >= amount - 1 else 0
    holding, spare = [largest] + [least] * (amount - 1), total - largest - least * (amount - 1)
    while spare > 0:
        candidates = [i for i in range(1, amount) if holding[i] < largest] or [i for i in range(1, amount) if holding[i] < reach]
        whole, remaining = sum([weights[i] for i in candidates]), spare
        for i in candidates:
            addition = min(reach - holding[i], max(1, remaining * weights[i] // whole), spare)
            holding[i] = holding[i] + addition
            spare = spare - addition
    return np.array(holding)


def gaussian(key, extent, scale, bound, split=(), kind=jnp.bfloat16):
    result = jax.random.normal(key, extent, jnp.float32) * scale
    if len(split) > 0:
        result = shard_levels(key, extent, split, -0.22, 0.18) * result
    return jnp.clip(result, min=-bound, max=bound).astype(kind)


def setup_inputs(seed: int = 0, part: int = 0) -> dict:
    keys = jax.random.split(jax.random.key(seed), 8)
    own_keys = jax.random.split(jax.random.fold_in(keys[7], part), 8)
    image = gaussian(own_keys[0], (V, ROWS, W), 1.0, 6.0, ((1, 16),), jnp.float32)
    inv_var = jnp.clip(jnp.exp(math.log(4.0) - 2.7725887 * jax.random.uniform(own_keys[1], (V, ROWS, W), jnp.float32) ** shard_levels(own_keys[1], (V, ROWS, W), ((1, 16),), -0.2, 0.2)), 0.25, 4.0)
    shift = jnp.clip(jax.random.uniform(own_keys[2], (V, 2), jnp.float32, -0.5, 0.5), -0.5, 0.5)
    col_offset = touch_ends(jax.random.randint(own_keys[3], (V,), -8, 9), jax.random.fold_in(own_keys[3], 1), -8, 8).astype(jnp.int32)
    psf_rows = gaussian(own_keys[4], (V, K, 41), 41 ** -0.5, 1.0, (), jnp.float32)
    psf_cols = gaussian(own_keys[5], (V, K, 41), (41 * K) ** -0.5, 0.5, (), jnp.float32)
    placement_keys = jax.random.split(jax.random.fold_in(own_keys[6], 1), PIECES // (V * (W // PC)))
    placement_turns = jax.random.permutation(jax.random.fold_in(own_keys[6], 3), PIECES // (V * (W // PC)))
    placement = jax.vmap(lambda own, number: routed_block(jax.random.fold_in(own_keys[6], 2), own, number, V * (W // PC), N_TILE, 1, CAP, 2))(placement_keys, placement_turns).reshape((PIECES, 1))
    return dict(image=image, inv_var=inv_var, shift=shift, col_offset=col_offset, psf_rows=psf_rows, psf_cols=psf_cols, placement=placement)


def lanczos(values):
    return jnp.where(jnp.abs(values) < 3.0, jnp.sinc(values) * jnp.sinc(values / 3.0), 0.0)


def tap_weights(fraction):
    places = jnp.arange(-3, 4).astype(jnp.float32)
    weights = lanczos(places[None, :] + fraction[:, None])
    return weights / jnp.sum(weights, axis=1, keepdims=True)


def warp(extended, shift, col_offset):
    height = extended.shape[1] - 6
    width = extended.shape[2]
    row_weight = tap_weights(shift[:, 0])
    col_weight = tap_weights(shift[:, 1])
    shifted = jnp.zeros((extended.shape[0], height, width), jnp.float32)
    for place in range(-3, 4):
        shifted = shifted + row_weight[:, place + 3, None, None] * extended[:, 3 - place:3 - place + height]
    padded = jnp.pad(shifted, ((0, 0), (0, 0), (11, 11)))

    def one_visit(plane, weights, offset):
        total = jnp.zeros((height, width), jnp.float32)
        for place in range(-3, 4):
            start = (11 - offset - place).astype(jnp.int32)
            total = total + weights[place + 3] * lax.dynamic_slice_in_dim(plane, start, width, 1)
        return total

    return jax.vmap(one_visit)(padded, col_weight, col_offset)


def match_psf(warped, psf_rows, psf_cols):
    height = warped.shape[1]
    width = warped.shape[2]
    padded_rows = jnp.pad(warped, ((0, 0), (20, 20), (0, 0)))
    matched = jnp.zeros(warped.shape, jnp.float32)
    for basis in range(psf_rows.shape[1]):
        along = jnp.zeros(warped.shape, jnp.float32)
        for place in range(41):
            along = along + psf_rows[:, basis, place, None, None] * padded_rows[:, 40 - place:40 - place + height]
        padded_cols = jnp.pad(along, ((0, 0), (0, 0), (20, 20)))
        for place in range(41):
            matched = matched + psf_cols[:, basis, place, None, None] * padded_cols[:, :, 40 - place:40 - place + width]
    return matched


def reference(image, inv_var, shift, col_offset, psf_rows, psf_cols, placement):
    warped = warp(jnp.pad(image, ((0, 0), (3, 3), (0, 0))), shift, col_offset)
    matched = match_psf(warped, psf_rows, psf_cols)
    visits = image.shape[0]
    width = image.shape[2]
    pieces = width // PC
    labels = placement.reshape(N_TILE, visits, pieces)
    owners = jnp.arange(N_TILE, dtype=jnp.int32)
    onehot = (labels[None] == owners[:, None, None, None]).astype(jnp.float32)
    weighted = (inv_var * matched).reshape(visits, N_TILE, RD, pieces, PC)
    weights = inv_var.reshape(visits, N_TILE, RD, pieces, PC)
    numer = jnp.einsum("pdvc,vdrcx->prx", onehot, weighted, precision=lax.Precision.HIGHEST)
    denom = jnp.einsum("pdvc,vdrcx->prx", onehot, weights, precision=lax.Precision.HIGHEST)
    return matched.astype(jnp.bfloat16), numer / jnp.maximum(denom, 1.0)
```

```python
import functools
import jax
import jax.numpy as jnp
from jax import lax
from jax.experimental import pallas as pl
from jax.experimental.pallas import tpu as pltpu
from jax.sharding import PartitionSpec as P

PC = 128
F32 = jnp.float32
BF16 = jnp.bfloat16
HIGHEST = lax.Precision.HIGHEST


def lanczos(values):
    return jnp.where(jnp.abs(values) < 3.0, jnp.sinc(values) * jnp.sinc(values / 3.0), 0.0)


def tap_weights(fraction):
    places = jnp.arange(-3, 4).astype(jnp.float32)
    weights = lanczos(places[None, :] + fraction[:, None])
    return weights / jnp.sum(weights, axis=1, keepdims=True)


def round_up(number, unit):
    return -(-number // unit) * unit


def split(x):
    high = x.astype(BF16)
    low = (x - high.astype(F32)).astype(BF16)
    return high, low


def band(vector, rows, lanes, shift):
    wide = vector.shape[-1]
    turned = pltpu.roll(jnp.broadcast_to(vector, (8, wide)), shift, 1)[:1]
    full = jnp.broadcast_to(turned, (rows, wide))
    return pltpu.roll(full, 0, 1, stride=1, stride_axis=0)[:, :lanes]


def prepare_kernel(
    bases, length, height, slots_ref, scal_ref, vecs_ref, inv_ref, rows_ref, cols_ref, edge_ref, den_ref
):
    visit = pl.program_id(0)
    half = length // 2
    ext = 3 * height
    pad = round_up(ext, 16)
    base = vecs_ref[0]
    psf = [band(base[k : k + 1, :PC], height, PC, height + half - (length - 1)) for k in range(bases)]
    psf = jnp.concatenate(psf, axis=0)
    warp = band(base[2 * bases : 2 * bases + 1, :PC], PC, PC, PC - 3)
    place = lax.broadcasted_iota(jnp.int32, (PC, PC), 0) + scal_ref[0] - height
    warp = jnp.where((place >= 0) & (place < scal_ref[1]), warp, 0.0)
    rows = jnp.dot(psf, warp, precision=HIGHEST, preferred_element_type=F32)
    lane = lax.broadcasted_iota(jnp.int32, rows.shape, 1)
    rows = jnp.where(lane < ext, rows, 0.0)
    high = rows.astype(BF16).astype(F32)
    low = rows - high
    blank = jnp.zeros_like(rows)
    high = jnp.concatenate([high, blank], axis=1)
    low = jnp.concatenate([low, blank], axis=1)
    rows_ref[0] = (high + pltpu.roll(low, pad, 1) + pltpu.roll(high, 2 * pad, 1)).astype(BF16)
    wide = 2 * PC
    psf = [
        band(base[bases + k : bases + k + 1], wide, PC, wide - (PC // 2 + half))
        for k in range(bases)
    ]
    warp = band(base[2 * bases + 1 : 2 * bases + 2], wide, wide, lax.rem(scal_ref[2 + visit] + wide - 3, wide))
    left_c = lax.broadcasted_iota(jnp.int32, (wide, wide), 0) < PC
    left_m = lax.broadcasted_iota(jnp.int32, (wide, wide), 1) < PC
    warp_edge = jnp.where(left_c == left_m, warp, 0.0)
    left_r = lax.broadcasted_iota(jnp.int32, (wide, PC), 0) < PC
    left_q = lax.broadcasted_iota(jnp.int32, (wide, PC), 1) < PC // 2
    for k in range(bases):
        for out, first, second in (
            (cols_ref, warp, psf[k]),
            (edge_ref, warp_edge, jnp.where(left_r == left_q, psf[k], 0.0)),
        ):
            both = jnp.dot(first, second, precision=HIGHEST, preferred_element_type=F32)
            high, low = split(both)
            out[0, k * wide : (k + 1) * wide, :PC] = high
            out[0, k * wide : (k + 1) * wide, PC:] = low

    @pl.when(visit == 0)
    def _():
        den_ref[...] = jnp.zeros_like(den_ref)

    pieces = inv_ref.shape[2] // PC
    for c in range(pieces):
        slot = slots_ref[visit * pieces + c]
        den_ref[slot] += inv_ref[0, :, c * PC : (c + 1) * PC]


def match_kernel(
    bases, first, last, slots_ref, up_ref, own_ref, down_ref, inv_ref, rows_ref, cols_ref, edge_ref,
    out_ref, send_ref, keep_ref, high_ref, low_ref, acc_ref
):
    step = pl.program_id(0)
    visit = step + first
    height, width = own_ref.shape[1], own_ref.shape[2]
    pieces = width // PC
    pairs = pieces // 2
    pad = round_up(3 * height, 16)
    deep = rows_ref.shape[2]
    operator = rows_ref[0]

    def columns(ref, pair):
        return [ref[0, :, n * PC : (n + 1) * PC] for n in (pair, pair + pairs)]

    def store(pair, along, order):
        for k in range(bases):
            block = [along[k * height : (k + 1) * height, h * PC : (h + 1) * PC] for h in order]
            high, low = split(jnp.concatenate(block, axis=0))
            high_ref[k, pair * 2 * height : (pair + 1) * 2 * height, :] = high
            low_ref[k, pair * 2 * height : (pair + 1) * 2 * height, :] = low

    for pair in range(pairs):
        parts = [columns(ref, pair) for ref in (up_ref, own_ref, down_ref)]
        stacked = jnp.concatenate([jnp.concatenate(part, axis=1) for part in parts], axis=0)
        if pad > 3 * height:
            stacked = jnp.concatenate([stacked, jnp.zeros((pad - 3 * height, 2 * PC), F32)], axis=0)
        high, low = split(stacked)
        depth = [high, high, low]
        if deep > 3 * pad:
            depth.append(jnp.zeros((deep - 3 * pad, 2 * PC), BF16))
        along = jnp.dot(operator, jnp.concatenate(depth, axis=0), preferred_element_type=F32)
        store(pair, along, (0, 1))
        if pair == 0:
            store(pairs, along, (1, 0))

    def window(ref, start, count):
        size = 2 * height
        parts = []
        for k in range(bases):
            for move in (0, 1):
                parts.append(ref[k, (start + move) * size : (start + move + count) * size, :])
        return jnp.concatenate(parts, axis=1)

    def blocks(start, count, weights_ref):
        high = jnp.dot(window(high_ref, start, count), weights_ref[0], preferred_element_type=F32)
        low = jnp.dot(window(low_ref, start, count), weights_ref[0, :, :PC], preferred_element_type=F32)
        return high[:, :PC] + high[:, PC:] + low

    main = blocks(0, pairs, cols_ref)
    edge = blocks(pairs - 1, 1, edge_ref)[height:]
    turned = [None] * pieces
    for n in range(pieces):
        row = (2 * (n % pairs) + n // pairs) * height
        block = main[row : row + height] if n < pieces - 1 else edge
        turned[n] = pltpu.roll(block, PC // 2, 1)
    lane = lax.broadcasted_iota(jnp.int32, (height, PC), 1)

    if first == 0:
        @pl.when(step == 0)
        def _():
            acc_ref[...] = jnp.zeros_like(acc_ref)

    for c in range(pieces):
        piece = jnp.where(lane < PC // 2, turned[c - 1], turned[c])
        span = slice(c * PC, (c + 1) * PC)
        out_ref[0, :, span] = piece.astype(BF16)
        slot = slots_ref[visit * pieces + c]
        acc_ref[slot] += inv_ref[0, :, span] * piece

    @pl.when(step == pl.num_programs(0) - 1)
    def _():
        count = acc_ref.shape[0] // 2
        keep_ref[...] = acc_ref[:count]
        send_ref[...] = acc_ref[count:]


def scatter_sum(keep, send, size):
    bit = 1
    while bit < size:
        pairs = [(i, i ^ bit) for i in range(size)]
        keep = keep + lax.ppermute(send, "tile", pairs)
        bit *= 2
        if bit < size:
            count = keep.shape[0] // 2
            keep, send = keep[:count], keep[count:]
    return keep


def on_device(image, inv_var, shift, col_offset, psf_rows, psf_cols, placement):
    visits, height, width = image.shape
    bases, length = psf_rows.shape[1:]
    size = lax.axis_size("tile")
    if size & (size - 1) or length // 2 + 3 > height or width % (2 * PC):
        raise ValueError("unsupported sizes")
    me = lax.axis_index("tile")
    pieces = width // PC
    rising = [(i, i + 1) for i in range(size - 1)]
    above = lax.ppermute(image, "tile", rising)
    below = lax.ppermute(image, "tile", [(j, i) for i, j in rising])

    relative = placement.reshape(-1) ^ me
    slots = jnp.zeros_like(relative)
    bits = size.bit_length() - 1
    for b in range(bits):
        slots = slots | (((relative >> b) & 1) << (bits - 1 - b))
    wide = 2 * PC

    def lanes(x):
        return jnp.pad(x, ((0, 0), (0, 0), (0, wide - x.shape[2])))

    row_tap = tap_weights(shift[:, 0])
    col_tap = tap_weights(shift[:, 1])
    vecs = jnp.concatenate(
        [
            lanes(psf_rows[:, :, ::-1]),
            lanes(psf_cols),
            lanes(row_tap[:, None, ::-1]),
            lanes(col_tap[:, None, :]),
        ],
        axis=1,
    )
    rank = vecs.shape[1]
    scal = jnp.concatenate(
        [jnp.stack([me * height, jnp.int32(size * height)]).astype(jnp.int32), col_offset]
    )
    deep = round_up(3 * round_up(3 * height, 16), 128)
    smem = pl.BlockSpec(memory_space=pltpu.SMEM)

    def per_visit(*shape):
        return pl.BlockSpec((1,) + shape, lambda v: (v,) + (0,) * len(shape))

    def whole(*shape):
        return pl.BlockSpec(shape, lambda v: (0,) * len(shape))

    rows_op, cols_op, edge_op, den = pl.pallas_call(
        functools.partial(prepare_kernel, bases, length, height),
        grid=(visits,),
        in_specs=[smem, smem, per_visit(rank, wide), per_visit(height, width)],
        out_specs=[
            per_visit(bases * height, deep),
            per_visit(bases * wide, wide),
            per_visit(bases * wide, wide),
            whole(size, height, PC),
        ],
        out_shape=[
            jax.ShapeDtypeStruct((visits, bases * height, deep), BF16),
            jax.ShapeDtypeStruct((visits, bases * wide, wide), BF16),
            jax.ShapeDtypeStruct((visits, bases * wide, wide), BF16),
            jax.ShapeDtypeStruct((size, height, PC), F32),
        ],
        name="prepare",
        cost_estimate=pl.CostEstimate(
            flops=visits * 12 * wide * wide * bases * PC, bytes_accessed=4 * visits * height * width, transcendentals=0
        ),
    )(slots, scal, vecs, inv_var)
    denom = scatter_sum(den[: size // 2], den[size // 2 :], size)

    pair_rows = (pieces + 2) * height
    half = (size // 2, height, PC)
    matched, send, keep = pl.pallas_call(
        functools.partial(match_kernel, bases, 0, True),
        grid=(visits,),
        in_specs=[smem]
        + [per_visit(height, width)] * 4
        + [per_visit(bases * height, deep)]
        + [per_visit(bases * wide, wide)] * 2,
        out_specs=[per_visit(height, width), whole(*half), whole(*half)],
        out_shape=[
            jax.ShapeDtypeStruct((visits, height, width), BF16),
            jax.ShapeDtypeStruct(half, F32),
            jax.ShapeDtypeStruct(half, F32),
        ],
        scratch_shapes=[
            pltpu.VMEM((bases, pair_rows, PC), BF16),
            pltpu.VMEM((bases, pair_rows, PC), BF16),
            pltpu.VMEM((size, height, PC), F32),
        ],
        name="match",
        cost_estimate=pl.CostEstimate(
            flops=visits * 6 * bases * height * width * 256, bytes_accessed=20 * visits * height * width, transcendentals=0
        ),
    )(slots, above, image, below, inv_var, rows_op, cols_op, edge_op)
    numer = scatter_sum(keep, send, size)
    return matched, numer / jnp.maximum(denom, 1.0)


def solution(mesh):
    in_specs = (
        P(None, ("groups", "tile"), None),
        P(None, ("groups", "tile"), None),
        P("groups", None),
        P("groups"),
        P("groups", None, None),
        P("groups", None, None),
        P(("groups", "tile"), None),
    )
    out_specs = (P(None, ("groups", "tile"), None), P(("groups", "tile"), None, None))
    return jax.shard_map(
        on_device, mesh=mesh, in_specs=in_specs, out_specs=out_specs, check_vma=False
    )
```

```python
import functools
import math
import jax
import jax.numpy as jnp
from jax import lax
from jax.experimental import pallas as pl
from jax.experimental.pallas import tpu as pltpu
from jax.sharding import PartitionSpec as P

PC = 128
WIDE = 2 * PC
TAPS = 3
F32 = jnp.float32
BF16 = jnp.bfloat16
HIGHEST = lax.Precision.HIGHEST
GRANT = 24 * 1024 * 1024


def round_up(number, unit):
    return -(-number // unit) * unit


def split(x):
    high = x.astype(BF16)
    low = (x - high.astype(F32)).astype(BF16)
    return high, low


def lane_of(shape):
    return lax.broadcasted_iota(jnp.int32, shape, len(shape) - 1)


def row_of(shape):
    return lax.broadcasted_iota(jnp.int32, shape, 0)


def sinc(u):
    angle = math.pi * u
    return jnp.where(u == 0.0, 1.0, jnp.sin(angle) / jnp.where(u == 0.0, 1.0, angle))


def tap_lanes(shift_ref):
    visits = shift_ref.shape[1]
    rows = round_up(2 * visits, 8)
    row, lane = row_of((rows, PC)), lane_of((rows, PC))
    fraction = jnp.zeros((rows, PC), F32)
    for r in range(2 * visits):
        fraction = jnp.where(row == r, shift_ref[r % 2, r // 2], fraction)
    u = (lane - TAPS).astype(F32) + fraction
    weight = jnp.where(jnp.abs(u) < 3.0, sinc(u) * sinc(u / 3.0), 0.0)
    weight = jnp.where(lane < 2 * TAPS + 1, weight, 0.0)
    return weight / jnp.sum(weight, axis=1, keepdims=True)


def band(vector, shift, rows=PC):
    wide = vector.shape[-1]
    turned = pltpu.roll(jnp.broadcast_to(vector, (8, wide)), shift, 1)[:1]
    full = jnp.broadcast_to(turned, (rows, wide))
    return pltpu.roll(full, 0, 1, stride=1, stride_axis=0)


def padded(block, rows, lanes):
    high, wide = block.shape
    block = jnp.concatenate([block, jnp.zeros((high, lanes - wide), F32)], axis=1)
    return jnp.concatenate([block, jnp.zeros((rows - high, lanes), F32)], axis=0)


def weights_kernel(order, place_ref, me_ref, inv_ref, keep_ref, send_ref, den_ref):
    visits, _, width = inv_ref.shape
    pieces = width // PC
    den_ref[...] = jnp.zeros_like(den_ref)
    for n in range(visits * pieces):
        slot = place_ref[n] ^ me_ref[0]
        span = slice(n % pieces * PC, (n % pieces + 1) * PC)
        den_ref[slot] += inv_ref[n // pieces, :, span]
    hand_out(order, den_ref, keep_ref, send_ref)


def hand_out(order, acc_ref, keep_ref, send_ref):
    half = len(order) // 2
    for i, slot in enumerate(order):
        if i < half:
            keep_ref[i, : acc_ref.shape[1]] = acc_ref[slot]
        else:
            send_ref[i - half] = acc_ref[slot]


def prepare_kernel(
    height, size, me_ref, shift_ref, offset_ref, psf_rows_ref, psf_cols_ref, rows_ref, cols_ref, edge_ref
):
    bases, visits, length = psf_rows_ref.shape
    half = length // 2
    ext = 3 * height
    pad = round_up(ext, 16)
    all_taps = tap_lanes(shift_ref)
    lane, row = lane_of((PC, PC)), row_of((PC, PC))
    left = lane < PC // 2
    place = lane + me_ref[0] * height - height
    inside = (place >= 0) & (place < size * height)
    for visit in range(visits):
        warp = jnp.where(inside, band(all_taps[2 * visit : 2 * visit + 1], PC - TAPS), 0.0)
        kernels = padded(psf_rows_ref[:, visit, :], 8, PC)
        psf = jnp.zeros((PC, PC), F32)
        for k in range(bases):
            one = jnp.where(lane < height, band(kernels[k : k + 1], PC - (height + half)), 0.0)
            psf = psf + (pltpu.roll(one, k * height, 1) if k else one)
        rows = jnp.dot(warp, psf, precision=HIGHEST, preferred_element_type=F32)
        rows = jnp.where(row < ext, rows, 0.0).T[: bases * height]
        high = rows.astype(BF16).astype(F32)
        low = rows - high
        blank = jnp.zeros_like(rows)
        high = jnp.concatenate([high, blank], axis=1)
        low = jnp.concatenate([low, blank], axis=1)
        rows_ref[visit] = (high + pltpu.roll(low, pad, 1) + pltpu.roll(high, 2 * pad, 1)).astype(BF16)
        taps = all_taps[2 * visit + 1 : 2 * visit + 2]
        offset = offset_ref[visit]
        kernels = padded(psf_cols_ref[:, visit, :], 8, PC)
        joined = jnp.zeros((8, PC), F32)
        for t in range(2 * TAPS + 1):
            weight = jnp.sum(jnp.where(lane[:8] == t, taps, 0.0), axis=1, keepdims=True)
            joined = joined + weight * pltpu.roll(kernels, (t - TAPS) % PC, 1)
        start = PC // 2 - half
        ends = []
        for k in range(bases):
            both = band(joined[k : k + 1], start + offset)
            for part, at in ((jnp.where(lane < row, both, 0.0), 0), (jnp.where(lane > row, both, 0.0), PC)):
                high, low = split(part)
                span = slice(k * WIDE + at, k * WIDE + at + PC)
                cols_ref[visit, span, :PC] = high
                cols_ref[visit, span, PC:] = low
            ends.append(jnp.where(left == (lane < row), band(kernels[k : k + 1], start), 0.0))
        far = jnp.concatenate([taps, jnp.zeros_like(taps)], axis=1)
        warp = band(far, lax.rem(offset + WIDE - TAPS, WIDE))[:, :PC]
        both = jnp.dot(warp, jnp.concatenate(ends, axis=1), precision=HIGHEST, preferred_element_type=F32)
        for k in range(bases):
            part = both[:, k * PC : (k + 1) * PC]
            for part, at in ((jnp.where(left, part, 0.0), 0), (jnp.where(left, 0.0, part), PC)):
                high, low = split(part)
                span = slice(k * WIDE + at, k * WIDE + at + PC)
                edge_ref[visit, span, :PC] = high
                edge_ref[visit, span, PC:] = low


def match_kernel(
    bases, first, last, order, place_ref, me_ref, fore_ref, back_ref, image_ref, inv_ref, rows_ref, cols_ref,
    edge_ref, *refs
):
    if first:
        old_ref, _, *refs = refs
    if last:
        mine_ref, other_ref, out_ref, keep_ref, send_ref, high_ref, low_ref, acc_ref = refs
    else:
        out_ref, acc_ref, high_ref, low_ref = refs
    step = pl.program_id(0)
    visit = step + first
    height, width = image_ref.shape[1:]
    pieces = width // PC
    pairs = pieces // 2
    pad = round_up(3 * height, 16)
    deep = rows_ref.shape[2]
    operator = rows_ref[visit]

    def column(n):
        span = slice(n * PC, (n + 1) * PC)
        parts = [fore_ref[step, :, span], image_ref[visit, :, span], back_ref[step, :, span]]
        if pad > 3 * height:
            parts.append(jnp.zeros((pad - 3 * height, PC), F32))
        return jnp.concatenate(parts, axis=0)

    def store(pair, along, turn):
        for k in range(bases):
            block = [along[k * height : (k + 1) * height, h * PC : (h + 1) * PC] for h in turn]
            high, low = split(jnp.concatenate(block, axis=0))
            high_ref[k, pair * 2 * height : (pair + 1) * 2 * height, :] = high
            low_ref[k, pair * 2 * height : (pair + 1) * 2 * height, :] = low

    for pair in range(pairs):
        stacked = jnp.concatenate([column(pair), column(pair + pairs)], axis=1)
        high, low = split(stacked)
        depth = [high, high, low]
        if deep > 3 * pad:
            depth.append(jnp.zeros((deep - 3 * pad, WIDE), BF16))
        along = jnp.dot(operator, jnp.concatenate(depth, axis=0), preferred_element_type=F32)
        store(pair, along, (0, 1))
        if pair == 0:
            store(pairs, along, (1, 0))

    def window(ref, start, count):
        size = 2 * height
        parts = []
        for k in range(bases):
            for move in (0, 1):
                parts.append(ref[k, (start + move) * size : (start + move + count) * size, :])
        return jnp.concatenate(parts, axis=1)

    def blocks(start, count, ref):
        high = jnp.dot(window(high_ref, start, count), ref[visit], preferred_element_type=F32)
        low = jnp.dot(window(low_ref, start, count), ref[visit, :, :PC], preferred_element_type=F32)
        return high[:, :PC] + high[:, PC:] + low

    main = blocks(0, pairs, cols_ref)
    edge = blocks(pairs - 1, 1, edge_ref)[height:]
    turned = [None] * pieces
    for n in range(pieces):
        row = (2 * (n % pairs) + n // pairs) * height
        block = main[row : row + height] if n < pieces - 1 else edge
        turned[n] = pltpu.roll(block, PC // 2, 1)
    lane = lane_of((height, PC))

    @pl.when(step == 0)
    def _():
        acc_ref[...] = old_ref[...] if first else jnp.zeros_like(acc_ref)

    for c in range(pieces):
        piece = jnp.where(lane < PC // 2, turned[c - 1], turned[c])
        span = slice(c * PC, (c + 1) * PC)
        out_ref[0, :, span] = piece.astype(BF16)
        slot = place_ref[visit * pieces + c] ^ me_ref[0]
        acc_ref[slot] += inv_ref[visit, :, span] * piece

    if last:
        @pl.when(step == pl.num_programs(0) - 1)
        def _():
            hand_out(order, acc_ref, keep_ref, send_ref)
            keep_ref[:, height:] = mine_ref[...] + other_ref[...]


def exchange(send, size, bit):
    return lax.ppermute(send, "tile", [(i, i ^ bit) for i in range(size)])


def on_device(image, inv_var, shift, col_offset, psf_rows, psf_cols, placement):
    visits, height, width = image.shape
    bases, length = psf_rows.shape[1:]
    size = lax.axis_size("tile")
    reach = length // 2 + TAPS
    if size & (size - 1) or reach > height or height % 8 or width % WIDE or visits < 3:
        raise ValueError("unsupported sizes")
    me = lax.axis_index("tile").astype(jnp.int32).reshape(1)
    place = placement.reshape(-1)
    bits = [1 << b for b in range(size.bit_length() - 1)]
    order = [0]
    for bit in reversed(bits):
        order = order + [slot ^ bit for slot in order]
    order = tuple(order)
    rising = [(i, i + 1) for i in range(size - 1)]
    falling = [(j, i) for i, j in rising]
    smem = pl.BlockSpec(memory_space=pltpu.SMEM)
    vmem = pl.BlockSpec(memory_space=pltpu.VMEM)
    anywhere = pl.BlockSpec(memory_space=pl.ANY)
    params = pltpu.CompilerParams(vmem_limit_bytes=GRANT)
    chunks = ((0, visits - 2), (visits - 2, 1), (visits - 1, 1))

    halos = []
    for (first, count) in chunks:
        part = image[first : first + count]
        fore = lax.ppermute(part, "tile", rising)
        back = lax.ppermute(part, "tile", falling)
        halos.append((fore, back))

    half = jax.ShapeDtypeStruct((size // 2, height, PC), F32)
    sums = pltpu.VMEM((size, height, PC), F32)
    weights = pl.pallas_call(
        functools.partial(weights_kernel, order),
        in_specs=[smem, smem, vmem],
        out_specs=[vmem, vmem],
        out_shape=[half, half],
        scratch_shapes=[sums],
        compiler_params=params,
        name="weights",
    )
    den = weights(place, me, inv_var)
    denom = (den[0], exchange(den[1], size, bits[0]))

    deep = round_up(3 * round_up(3 * height, 16), 128)
    prepare = pl.pallas_call(
        functools.partial(prepare_kernel, height, size),
        in_specs=[smem, smem, smem, vmem, vmem],
        out_specs=[vmem] * 3,
        out_shape=[
            jax.ShapeDtypeStruct((visits, bases * height, deep), BF16),
            jax.ShapeDtypeStruct((visits, bases * WIDE, WIDE), BF16),
            jax.ShapeDtypeStruct((visits, bases * WIDE, WIDE), BF16),
        ],
        compiler_params=params,
        name="prepare",
    )
    operators = prepare(
        me, shift.T, col_offset, psf_rows.transpose(1, 0, 2), psf_cols.transpose(1, 0, 2)
    )

    carried = ()
    for (first, count), (fore, back) in zip(chunks, halos):
        last = first + count == visits
        shapes = [jax.ShapeDtypeStruct((visits, height, width), BF16)]
        specs = [pl.BlockSpec((1, height, width), lambda v, first=first: (v + first, 0, 0))]
        pair_rows = (width // PC + 2) * height
        scratch = [pltpu.VMEM((bases, pair_rows, PC), BF16)] * 2
        inputs = [vmem] * 7
        extra = []
        if first:
            inputs += [vmem, anywhere]
            extra += [carried[1], carried[0]]
        if last:
            inputs += [vmem, vmem]
            extra += denom
            shapes += [jax.ShapeDtypeStruct((size // 2, 2 * height, PC), F32), half]
            specs += [vmem, vmem]
            scratch += [sums]
        else:
            shapes += [jax.ShapeDtypeStruct((size, height, PC), F32)]
            specs += [vmem]
        match = pl.pallas_call(
            functools.partial(match_kernel, bases, first, last, order),
            grid=(count,),
            in_specs=[smem, smem] + inputs,
            out_specs=specs,
            out_shape=shapes,
            scratch_shapes=scratch,
            input_output_aliases={10: 0} if first else {},
            compiler_params=params,
            cost_estimate=pl.CostEstimate(
                flops=count * 6 * bases * height * width * WIDE,
                bytes_accessed=20 * count * height * width,
                transcendentals=0,
            ),
        )
        carried = match(place, me, fore, back, image, inv_var, *operators, *extra)
    matched, keep, send = carried
    received = exchange(send, size, bits[0])
    keep = jnp.concatenate([keep[:, :height] + received, keep[:, height:]], axis=1)
    for bit in bits[1:]:
        count = keep.shape[0] // 2
        keep = keep[:count] + exchange(keep[count:], size, bit)
    return matched, keep[:, :height] / jnp.maximum(keep[:, height:], 1.0)


def solution(mesh):
    in_specs = (
        P(None, ("groups", "tile"), None),
        P(None, ("groups", "tile"), None),
        P("groups", None),
        P("groups"),
        P("groups", None, None),
        P("groups", None, None),
        P(("groups", "tile"), None),
    )
    out_specs = (P(None, ("groups", "tile"), None), P(("groups", "tile"), None, None))

    return jax.shard_map(
        on_device, mesh=mesh, in_specs=in_specs, out_specs=out_specs, check_vma=False
    )
```

```python
import functools
import math
import jax
import jax.numpy as jnp
from jax import lax
from jax.experimental import pallas as pl
from jax.experimental.pallas import tpu as pltpu
from jax.sharding import PartitionSpec as P

PC = 128
WIDE = 2 * PC
TAPS = 3
F32 = jnp.float32
BF16 = jnp.bfloat16
HIGHEST = lax.Precision.HIGHEST
GRANT = 24 * 1024 * 1024
GROUPS = 2


def round_up(number, unit):
    return -(-number // unit) * unit


def split(x):
    high = x.astype(BF16)
    low = (x - high.astype(F32)).astype(BF16)
    return high, low


def lane_of(shape):
    return lax.broadcasted_iota(jnp.int32, shape, len(shape) - 1)


def row_of(shape):
    return lax.broadcasted_iota(jnp.int32, shape, 0)


def sinc(u):
    angle = math.pi * u
    return jnp.where(u == 0.0, 1.0, jnp.sin(angle) / jnp.where(u == 0.0, 1.0, angle))


def tap_lanes(shift_ref):
    visits = shift_ref.shape[1]
    rows = round_up(2 * visits, 8)
    row, lane = row_of((rows, PC)), lane_of((rows, PC))
    fraction = jnp.zeros((rows, PC), F32)
    for r in range(2 * visits):
        fraction = jnp.where(row == r, shift_ref[r % 2, r // 2], fraction)
    u = (lane - TAPS).astype(F32) + fraction
    weight = jnp.where(jnp.abs(u) < 3.0, sinc(u) * sinc(u / 3.0), 0.0)
    weight = jnp.where(lane < 2 * TAPS + 1, weight, 0.0)
    return weight / jnp.sum(weight, axis=1, keepdims=True)


def band(vector, shift, rows=PC):
    wide = vector.shape[-1]
    turned = pltpu.roll(jnp.broadcast_to(vector, (8, wide)), shift, 1)[:1]
    full = jnp.broadcast_to(turned, (rows, wide))
    return pltpu.roll(full, 0, 1, stride=1, stride_axis=0)


def padded(block, rows, lanes):
    high, wide = block.shape
    block = jnp.concatenate([block, jnp.zeros((high, lanes - wide), F32)], axis=1)
    return jnp.concatenate([block, jnp.zeros((rows - high, lanes), F32)], axis=0)


def pack_kernel(image_ref, fore_ref, back_ref):
    height, width = image_ref.shape[1:]
    tail = width // 8
    body = width - tail
    sub = row_of((8, tail))
    for ref, row, spare in ((fore_ref, 0, 0), (back_ref, height - 8, 7)):
        ends = image_ref[0, row : row + 8, body:]
        packed = []
        for j, r in enumerate(r for r in range(8) if r != spare):
            moved = pltpu.roll(ends, (spare - r) % 8, 0)
            part = image_ref[0, row : row + 8, j * tail : (j + 1) * tail]
            packed.append(jnp.where(sub == spare, moved, part))
        incomplete = [jnp.concatenate(packed, axis=1)]
        full = [image_ref[0, t : t + 8, :] for t in range(0, height, 8) if t != row]
        lanes = 0
        for part in incomplete + full if row == 0 else full + incomplete:
            ref[0, :, lanes : lanes + part.shape[1]] = part
            lanes += part.shape[1]


def weights_kernel(order, place_ref, inv_ref, keep_ref, send_ref, den_ref):
    visits, _, width = inv_ref.shape
    pieces = width // PC
    den_ref[...] = jnp.zeros_like(den_ref)
    for n in range(visits * pieces):
        slot = place_ref[n]
        span = slice(n % pieces * PC, (n % pieces + 1) * PC)
        den_ref[n % 2, slot] += inv_ref[n // pieces, :, span]
    hand_out(order, den_ref, keep_ref, send_ref)


def hand_out(order, acc_ref, keep_ref, send_ref):
    half = len(order) // 2
    for i, slot in enumerate(order):
        total = acc_ref[0, slot] + acc_ref[1, slot]
        if i < half:
            keep_ref[i, : acc_ref.shape[2]] = total
        else:
            send_ref[i - half] = total


def prepare_kernel(
    height, size, me_ref, shift_ref, offset_ref, psf_rows_ref, psf_cols_ref, rows_ref, cols_ref, edge_ref
):
    bases, visits, length = psf_rows_ref.shape
    half = length // 2
    ext = 3 * height
    pad = round_up(ext, 16)
    all_taps = tap_lanes(shift_ref)
    lane, row = lane_of((PC, PC)), row_of((PC, PC))
    left = lane < PC // 2
    place = lane + me_ref[0] * height - height
    inside = (place >= 0) & (place < size * height)
    for visit in range(visits):
        warp = jnp.where(inside, band(all_taps[2 * visit : 2 * visit + 1], PC - TAPS), 0.0)
        kernels = padded(psf_rows_ref[:, visit, :], 8, PC)
        psf = jnp.zeros((PC, PC), F32)
        for k in range(bases):
            one = jnp.where(lane < height, band(kernels[k : k + 1], PC - (height + half)), 0.0)
            psf = psf + (pltpu.roll(one, k * height, 1) if k else one)
        rows = jnp.dot(warp, psf, precision=HIGHEST, preferred_element_type=F32)
        rows = jnp.where(row < ext, rows, 0.0).T[: bases * height]
        high = rows.astype(BF16).astype(F32)
        low = rows - high
        blank = jnp.zeros_like(rows)
        high = jnp.concatenate([high, blank], axis=1)
        low = jnp.concatenate([low, blank], axis=1)
        rows_ref[visit] = (high + pltpu.roll(low, pad, 1) + pltpu.roll(high, 2 * pad, 1)).astype(BF16)
        taps = all_taps[2 * visit + 1 : 2 * visit + 2]
        offset = offset_ref[visit]
        kernels = padded(psf_cols_ref[:, visit, :], 8, PC)
        joined = jnp.zeros((8, PC), F32)
        for t in range(2 * TAPS + 1):
            weight = jnp.sum(jnp.where(lane[:8] == t, taps, 0.0), axis=1, keepdims=True)
            joined = joined + weight * pltpu.roll(kernels, (t - TAPS) % PC, 1)
        start = PC // 2 - half
        ends = []
        for k in range(bases):
            both = band(joined[k : k + 1], start + offset)
            for part, at in ((jnp.where(lane < row, both, 0.0), 0), (jnp.where(lane > row, both, 0.0), PC)):
                high, low = split(part)
                span = slice(k * WIDE + at, k * WIDE + at + PC)
                cols_ref[visit, span, :PC] = high
                cols_ref[visit, span, PC:] = low
            ends.append(jnp.where(left == (lane < row), band(kernels[k : k + 1], start), 0.0))
        far = jnp.concatenate([taps, jnp.zeros_like(taps)], axis=1)
        warp = band(far, lax.rem(offset + WIDE - TAPS, WIDE))[:, :PC]
        both = jnp.dot(warp, jnp.concatenate(ends, axis=1), precision=HIGHEST, preferred_element_type=F32)
        for k in range(bases):
            part = both[:, k * PC : (k + 1) * PC]
            for part, at in ((jnp.where(left, part, 0.0), 0), (jnp.where(left, 0.0, part), PC)):
                high, low = split(part)
                span = slice(k * WIDE + at, k * WIDE + at + PC)
                edge_ref[visit, span, :PC] = high
                edge_ref[visit, span, PC:] = low


def match_kernel(
    bases, first, last, order, place_ref, fore_ref, back_ref, image_ref, inv_ref, rows_ref, cols_ref,
    edge_ref, *refs
):
    if first:
        old_ref, _, *refs = refs
    if last:
        mine_ref, other_ref, out_ref, keep_ref, send_ref, high_ref, low_ref, acc_ref = refs
    else:
        out_ref, acc_ref, high_ref, low_ref = refs
    step = pl.program_id(0)
    visit = step + first
    height, width = image_ref.shape[1:]
    pieces = width // PC
    pairs = pieces // 2
    pad = round_up(3 * height, 16)
    deep = rows_ref.shape[2]
    operator = rows_ref[visit]
    tail = width // 8
    body = width - tail
    split_at = body // PC

    def unpacked(ref, n, base, spare):
        if n < split_at:
            return ref[step, :, base + n * PC : base + (n + 1) * PC]
        parts = []
        for r in range(8):
            j = r - (r > spare)
            at = base + j * tail + (n - split_at) * PC
            if r == spare:
                parts.append(jnp.zeros((1, PC), F32))
            else:
                parts.append(ref[step, spare : spare + 1, at : at + PC])
        return jnp.concatenate(parts, axis=0)

    def column(n):
        full = height // 8 - 1
        parts = [unpacked(fore_ref, n, 0, 0)]
        for t in range(full):
            at = body + t * width + n * PC
            parts.append(fore_ref[step, :, at : at + PC])
        parts.append(image_ref[visit, :, n * PC : (n + 1) * PC])
        for t in range(full):
            at = t * width + n * PC
            parts.append(back_ref[step, :, at : at + PC])
        parts.append(unpacked(back_ref, n, full * width, 7))
        if pad > 3 * height:
            parts.append(jnp.zeros((pad - 3 * height, PC), F32))
        return jnp.concatenate(parts, axis=0)

    def store(pair, along, turn):
        for k in range(bases):
            block = [along[k * height : (k + 1) * height, h * PC : (h + 1) * PC] for h in turn]
            high, low = split(jnp.concatenate(block, axis=0))
            high_ref[k, pair * 2 * height : (pair + 1) * 2 * height, :] = high
            low_ref[k, pair * 2 * height : (pair + 1) * 2 * height, :] = low

    def fill(pair):
        stacked = jnp.concatenate([column(pair), column(pair + pairs)], axis=1)
        high, low = split(stacked)
        depth = [high, high, low]
        if deep > 3 * pad:
            depth.append(jnp.zeros((deep - 3 * pad, WIDE), BF16))
        along = jnp.dot(operator, jnp.concatenate(depth, axis=0), preferred_element_type=F32)
        store(pair, along, (0, 1))
        if pair == 0:
            store(pairs, along, (1, 0))

    def window(ref, start, count):
        size = 2 * height
        parts = []
        for k in range(bases):
            for move in (0, 1):
                parts.append(ref[k, (start + move) * size : (start + move + count) * size, :])
        return jnp.concatenate(parts, axis=1)

    def blocks(start, count, ref):
        high = jnp.dot(window(high_ref, start, count), ref[visit], preferred_element_type=F32)
        low = jnp.dot(window(low_ref, start, count), ref[visit, :, :PC], preferred_element_type=F32)
        return high[:, :PC] + high[:, PC:] + low

    @pl.when(step == 0)
    def _():
        acc_ref[...] = old_ref[...] if first else jnp.zeros_like(acc_ref)

    lane = lane_of((height, PC))
    turned = {}
    done = set()

    def finish():
        for c in range(pieces):
            if c in done or c not in turned or (c - 1) % pieces not in turned:
                continue
            done.add(c)
            piece = jnp.where(lane < PC // 2, turned[(c - 1) % pieces], turned[c])
            span = slice(c * PC, (c + 1) * PC)
            out_ref[0, :, span] = piece.astype(BF16)
            slot = place_ref[visit * pieces + c]
            acc_ref[c % 2, slot] += inv_ref[visit, :, span] * piece

    for pair in range(min(pairs, pairs // GROUPS + 1)):
        fill(pair)
    for group in range(GROUPS):
        start, count = group * pairs // GROUPS, pairs // GROUPS
        main = blocks(start, count, cols_ref)
        for pair in range(start + count + 1, min(pairs, start + 2 * count + 1)):
            fill(pair)
        if group == GROUPS - 1:
            edge = blocks(pairs - 1, 1, edge_ref)[height:]
        for pair in range(start, start + count):
            for h in (0, 1):
                n = pair + h * pairs
                row = (2 * (pair - start) + h) * height
                block = main[row : row + height] if n < pieces - 1 else edge
                turned[n] = pltpu.roll(block, PC // 2, 1)
        finish()

    if last:
        @pl.when(step == pl.num_programs(0) - 1)
        def _():
            hand_out(order, acc_ref, keep_ref, send_ref)
            keep_ref[:, height:] = mine_ref[...] + other_ref[...]


def exchange(send, size, bit):
    return lax.ppermute(send, "tile", [(i, i ^ bit) for i in range(size)])


def on_device(image, inv_var, shift, col_offset, psf_rows, psf_cols, placement):
    visits, height, width = image.shape
    bases, length = psf_rows.shape[1:]
    size = lax.axis_size("tile")
    reach = length // 2 + TAPS
    if size & (size - 1) or reach != height - 1 or height % 8 or width % (8 * PC) or visits < 3:
        raise ValueError("unsupported sizes")
    index = lax.axis_index("tile").astype(jnp.int32)
    place = placement.reshape(-1) ^ index
    me = index.reshape(1)
    bits = [1 << b for b in range(size.bit_length() - 1)]
    order = [0]
    for bit in reversed(bits):
        order = order + [slot ^ bit for slot in order]
    order = tuple(order)
    rising = [(i, i + 1) for i in range(size - 1)]
    falling = [(j, i) for i, j in rising]
    smem = pl.BlockSpec(memory_space=pltpu.SMEM)
    vmem = pl.BlockSpec(memory_space=pltpu.VMEM)
    anywhere = pl.BlockSpec(memory_space=pl.ANY)
    params = pltpu.CompilerParams(vmem_limit_bytes=GRANT)
    lanes = height * width // 8 - width // 8
    chunks = ((0, visits - 2), (visits - 2, 1), (visits - 1, 1))

    halos = []
    for (first, count) in chunks:
        block = pl.BlockSpec((1, 8, lanes), lambda v: (v, 0, 0))
        fore, back = pl.pallas_call(
            pack_kernel,
            grid=(count,),
            in_specs=[pl.BlockSpec((1, height, width), lambda v, first=first: (v + first, 0, 0))],
            out_specs=[block] * 2,
            out_shape=[jax.ShapeDtypeStruct((count, 8, lanes), F32)] * 2,
            compiler_params=pltpu.CompilerParams(vmem_limit_bytes=60 * 1024 * 1024),
        )(image)
        fore = lax.ppermute(fore, "tile", rising)
        back = lax.ppermute(back, "tile", falling)
        halos.append((fore, back))

    half = jax.ShapeDtypeStruct((size // 2, height, PC), F32)
    sums = pltpu.VMEM((2, size, height, PC), F32)
    weights = pl.pallas_call(
        functools.partial(weights_kernel, order),
        in_specs=[smem, vmem],
        out_specs=[vmem, vmem],
        out_shape=[half, half],
        scratch_shapes=[sums],
        compiler_params=params,
        name="weights",
    )
    den = weights(place, inv_var)
    denom = (den[0], exchange(den[1], size, bits[0]))

    deep = round_up(3 * round_up(3 * height, 16), 128)
    prepare = pl.pallas_call(
        functools.partial(prepare_kernel, height, size),
        in_specs=[smem, smem, smem, vmem, vmem],
        out_specs=[vmem] * 3,
        out_shape=[
            jax.ShapeDtypeStruct((visits, bases * height, deep), BF16),
            jax.ShapeDtypeStruct((visits, bases * WIDE, WIDE), BF16),
            jax.ShapeDtypeStruct((visits, bases * WIDE, WIDE), BF16),
        ],
        compiler_params=params,
        name="prepare",
    )
    operators = prepare(
        me, shift.T, col_offset, psf_rows.transpose(1, 0, 2), psf_cols.transpose(1, 0, 2)
    )

    carried = ()
    for (first, count), (fore, back) in zip(chunks, halos):
        last = first + count == visits
        shapes = [jax.ShapeDtypeStruct((visits, height, width), BF16)]
        specs = [pl.BlockSpec((1, height, width), lambda v, first=first: (v + first, 0, 0))]
        pair_rows = (width // PC + 2) * height
        scratch = [pltpu.VMEM((bases, pair_rows, PC), BF16)] * 2
        inputs = [vmem] * 7
        extra = []
        if first:
            inputs += [vmem, anywhere]
            extra += [carried[1], carried[0]]
        if last:
            inputs += [vmem, vmem]
            extra += denom
            shapes += [jax.ShapeDtypeStruct((size // 2, 2 * height, PC), F32), half]
            specs += [vmem, vmem]
            scratch += [sums]
        else:
            shapes += [jax.ShapeDtypeStruct((2, size, height, PC), F32)]
            specs += [vmem]
        match = pl.pallas_call(
            functools.partial(match_kernel, bases, first, last, order),
            grid=(count,),
            in_specs=[smem] + inputs,
            out_specs=specs,
            out_shape=shapes,
            scratch_shapes=scratch,
            input_output_aliases={9: 0} if first else {},
            compiler_params=params,
            cost_estimate=pl.CostEstimate(
                flops=count * 6 * bases * height * width * WIDE,
                bytes_accessed=20 * count * height * width,
                transcendentals=0,
            ),
        )
        carried = match(place, fore, back, image, inv_var, *operators, *extra)
    matched, keep, send = carried
    received = exchange(send, size, bits[0])
    keep = jnp.concatenate([keep[:, :height] + received, keep[:, height:]], axis=1)
    rest = bits[1:]
    while rest:
        near, rest = rest[:2], rest[2:]
        masks = [0, near[1], near[0], sum(near)] if len(near) > 1 else [0, near[0]]
        count = keep.shape[0] // len(masks)
        parts = {mask: keep[i * count : (i + 1) * count] for i, mask in enumerate(masks)}
        total = parts[0]
        for mask in sorted(parts, reverse=True)[:-1]:
            total = total + exchange(parts[mask], size, mask)
        keep = total
    return matched, keep[:, :height] / jnp.maximum(keep[:, height:], 1.0)


def solution(mesh):
    in_specs = (
        P(None, ("groups", "tile"), None),
        P(None, ("groups", "tile"), None),
        P("groups", None),
        P("groups"),
        P("groups", None, None),
        P("groups", None, None),
        P(("groups", "tile"), None),
    )
    out_specs = (P(None, ("groups", "tile"), None), P(("groups", "tile"), None, None))

    return jax.shard_map(
        on_device, mesh=mesh, in_specs=in_specs, out_specs=out_specs, check_vma=False
    )
```

```python
import functools
import math
import jax
import jax.numpy as jnp
from jax import lax
from jax.experimental import pallas as pl
from jax.experimental.pallas import tpu as pltpu
from jax.sharding import PartitionSpec as P

PC = 128
WIDE = 2 * PC
TAPS = 3
F32 = jnp.float32
BF16 = jnp.bfloat16
HIGHEST = lax.Precision.HIGHEST
GRANT = 24 * 1024 * 1024
GROUPS = 2


def round_up(number, unit):
    return -(-number // unit) * unit


def split(x):
    high = x.astype(BF16)
    low = (x - high.astype(F32)).astype(BF16)
    return high, low


def lane_of(shape):
    return lax.broadcasted_iota(jnp.int32, shape, len(shape) - 1)


def row_of(shape):
    return lax.broadcasted_iota(jnp.int32, shape, 0)


def sinc(u):
    angle = math.pi * u
    return jnp.where(u == 0.0, 1.0, jnp.sin(angle) / jnp.where(u == 0.0, 1.0, angle))


def tap_lanes(shift_ref):
    visits = shift_ref.shape[1]
    rows = round_up(2 * visits, 8)
    row, lane = row_of((rows, PC)), lane_of((rows, PC))
    fraction = jnp.zeros((rows, PC), F32)
    for r in range(2 * visits):
        fraction = jnp.where(row == r, shift_ref[r % 2, r // 2], fraction)
    u = (lane - TAPS).astype(F32) + fraction
    weight = jnp.where(jnp.abs(u) < 3.0, sinc(u) * sinc(u / 3.0), 0.0)
    weight = jnp.where(lane < 2 * TAPS + 1, weight, 0.0)
    return weight / jnp.sum(weight, axis=1, keepdims=True)


def band(vector, shift, rows=PC):
    wide = vector.shape[-1]
    turned = pltpu.roll(jnp.broadcast_to(vector, (8, wide)), shift, 1)[:1]
    full = jnp.broadcast_to(turned, (rows, wide))
    return pltpu.roll(full, 0, 1, stride=1, stride_axis=0)


def padded(block, rows, lanes):
    high, wide = block.shape
    block = jnp.concatenate([block, jnp.zeros((high, lanes - wide), F32)], axis=1)
    return jnp.concatenate([block, jnp.zeros((rows - high, lanes), F32)], axis=0)


def pack_kernel(me_ref, image_ref, far_ref, near_ref):
    height, width = image_ref.shape[1:]
    tail = width // 8
    body = width - tail
    sub = row_of((8, tail))
    tiles = [image_ref[0, t : t + 8, :] for t in range(0, height, 8)]

    def fill(ref, incomplete, full):
        ends = incomplete[:, body:]
        packed = []
        for r in range(1, 8):
            part = incomplete[:, (r - 1) * tail : r * tail]
            packed.append(jnp.where(sub == 0, pltpu.roll(ends, 8 - r, 0), part))
        lanes = 0
        for part in [jnp.concatenate(packed, axis=1)] + full:
            ref[0, :, lanes : lanes + part.shape[1]] = part
            lanes += part.shape[1]

    def both(after_ref, before_ref):
        fill(after_ref, tiles[0], tiles[1:])
        fill(before_ref, pltpu.roll(tiles[-1], 1, 0), tiles[:-1])

    odd = lax.rem(me_ref[0], 2)
    pl.when(odd == 1)(lambda: both(far_ref, near_ref))
    pl.when(odd == 0)(lambda: both(near_ref, far_ref))


def weights_kernel(order, place_ref, inv_ref, keep_ref, send_ref, den_ref):
    visits, _, width = inv_ref.shape
    pieces = width // PC
    den_ref[...] = jnp.zeros_like(den_ref)
    for n in range(visits * pieces):
        slot = place_ref[n]
        span = slice(n % pieces * PC, (n % pieces + 1) * PC)
        den_ref[n % 2, slot] += inv_ref[n // pieces, :, span]
    hand_out(order, den_ref, keep_ref, send_ref)


def hand_out(order, acc_ref, keep_ref, send_ref):
    half = len(order) // 2
    for i, slot in enumerate(order):
        total = acc_ref[0, slot] + acc_ref[1, slot]
        if i < half:
            keep_ref[i, : acc_ref.shape[2]] = total
        else:
            send_ref[i - half] = total


def prepare_kernel(
    height, size, me_ref, shift_ref, offset_ref, psf_rows_ref, psf_cols_ref, rows_ref, cols_ref, edge_ref
):
    bases, visits, length = psf_rows_ref.shape
    half = length // 2
    ext = 3 * height
    pad = round_up(ext, 16)
    all_taps = tap_lanes(shift_ref)
    lane, row = lane_of((PC, PC)), row_of((PC, PC))
    left = lane < PC // 2
    place = lane + me_ref[0] * height - height
    inside = (place >= 0) & (place < size * height)
    for visit in range(visits):
        warp = jnp.where(inside, band(all_taps[2 * visit : 2 * visit + 1], PC - TAPS), 0.0)
        kernels = padded(psf_rows_ref[:, visit, :], 8, PC)
        psf = jnp.zeros((PC, PC), F32)
        for k in range(bases):
            one = jnp.where(lane < height, band(kernels[k : k + 1], PC - (height + half)), 0.0)
            psf = psf + (pltpu.roll(one, k * height, 1) if k else one)
        rows = jnp.dot(warp, psf, precision=HIGHEST, preferred_element_type=F32)
        above = rows[:height]
        below = [pltpu.roll(rows[ext - 8 : ext], 1, 0), rows[2 * height : ext - 8]]
        below = jnp.concatenate(below, axis=0)
        odd = lax.rem(me_ref[0], 2) == 1
        rows = jnp.concatenate(
            [
                jnp.where(odd, below, above),
                rows[height : 2 * height],
                jnp.where(odd, above, below),
                jnp.zeros((PC - ext, PC), F32),
            ],
            axis=0,
        ).T[: bases * height]
        high = rows.astype(BF16).astype(F32)
        low = rows - high
        blank = jnp.zeros_like(rows)
        high = jnp.concatenate([high, blank], axis=1)
        low = jnp.concatenate([low, blank], axis=1)
        rows_ref[visit] = (high + pltpu.roll(low, pad, 1) + pltpu.roll(high, 2 * pad, 1)).astype(BF16)
        taps = all_taps[2 * visit + 1 : 2 * visit + 2]
        offset = offset_ref[visit]
        kernels = padded(psf_cols_ref[:, visit, :], 8, PC)
        joined = jnp.zeros((8, PC), F32)
        for t in range(2 * TAPS + 1):
            weight = jnp.sum(jnp.where(lane[:8] == t, taps, 0.0), axis=1, keepdims=True)
            joined = joined + weight * pltpu.roll(kernels, (t - TAPS) % PC, 1)
        start = PC // 2 - half
        ends = []
        for k in range(bases):
            both = band(joined[k : k + 1], start + offset)
            for part, at in ((jnp.where(lane < row, both, 0.0), 0), (jnp.where(lane > row, both, 0.0), PC)):
                high, low = split(part)
                span = slice(k * WIDE + at, k * WIDE + at + PC)
                cols_ref[visit, span, :PC] = high
                cols_ref[visit, span, PC:] = low
            ends.append(jnp.where(left == (lane < row), band(kernels[k : k + 1], start), 0.0))
        far = jnp.concatenate([taps, jnp.zeros_like(taps)], axis=1)
        warp = band(far, lax.rem(offset + WIDE - TAPS, WIDE))[:, :PC]
        both = jnp.dot(warp, jnp.concatenate(ends, axis=1), precision=HIGHEST, preferred_element_type=F32)
        for k in range(bases):
            part = both[:, k * PC : (k + 1) * PC]
            for part, at in ((jnp.where(left, part, 0.0), 0), (jnp.where(left, 0.0, part), PC)):
                high, low = split(part)
                span = slice(k * WIDE + at, k * WIDE + at + PC)
                edge_ref[visit, span, :PC] = high
                edge_ref[visit, span, PC:] = low


def match_kernel(
    bases, first, last, order, place_ref, far_ref, near_ref, image_ref, inv_ref, rows_ref, cols_ref,
    edge_ref, *refs
):
    if first:
        old_ref, _, *refs = refs
    if last:
        mine_ref, other_ref, out_ref, keep_ref, send_ref, high_ref, low_ref, acc_ref = refs
    else:
        out_ref, acc_ref, high_ref, low_ref = refs
    step = pl.program_id(0)
    visit = step + first
    height, width = image_ref.shape[1:]
    pieces = width // PC
    pairs = pieces // 2
    pad = round_up(3 * height, 16)
    deep = rows_ref.shape[2]
    operator = rows_ref[visit]
    tail = width // 8
    body = width - tail
    split_at = body // PC

    def halo(ref, n):
        if n < split_at:
            parts = [ref[step, :, n * PC : (n + 1) * PC]]
        else:
            parts = [jnp.zeros((1, PC), F32)]
            for r in range(1, 8):
                at = (r - 1) * tail + (n - split_at) * PC
                parts.append(ref[step, 0:1, at : at + PC])
        for t in range(height // 8 - 1):
            at = body + t * width + n * PC
            parts.append(ref[step, :, at : at + PC])
        return parts

    def column(n):
        parts = halo(far_ref, n) + [image_ref[visit, :, n * PC : (n + 1) * PC]] + halo(near_ref, n)
        if pad > 3 * height:
            parts.append(jnp.zeros((pad - 3 * height, PC), F32))
        return jnp.concatenate(parts, axis=0)

    def store(pair, along, turn):
        for k in range(bases):
            block = [along[k * height : (k + 1) * height, h * PC : (h + 1) * PC] for h in turn]
            high, low = split(jnp.concatenate(block, axis=0))
            high_ref[k, pair * 2 * height : (pair + 1) * 2 * height, :] = high
            low_ref[k, pair * 2 * height : (pair + 1) * 2 * height, :] = low

    def fill(pair):
        stacked = jnp.concatenate([column(pair), column(pair + pairs)], axis=1)
        high, low = split(stacked)
        depth = [high, high, low]
        if deep > 3 * pad:
            depth.append(jnp.zeros((deep - 3 * pad, WIDE), BF16))
        along = jnp.dot(operator, jnp.concatenate(depth, axis=0), preferred_element_type=F32)
        store(pair, along, (0, 1))
        if pair == 0:
            store(pairs, along, (1, 0))

    def window(ref, start, count):
        size = 2 * height
        parts = []
        for k in range(bases):
            for move in (0, 1):
                parts.append(ref[k, (start + move) * size : (start + move + count) * size, :])
        return jnp.concatenate(parts, axis=1)

    def blocks(start, count, ref):
        high = jnp.dot(window(high_ref, start, count), ref[visit], preferred_element_type=F32)
        low = jnp.dot(window(low_ref, start, count), ref[visit, :, :PC], preferred_element_type=F32)
        return high[:, :PC] + high[:, PC:] + low

    @pl.when(step == 0)
    def _():
        acc_ref[...] = old_ref[...] if first else jnp.zeros_like(acc_ref)

    lane = lane_of((height, PC))
    turned = {}
    done = set()

    def finish():
        for c in range(pieces):
            if c in done or c not in turned or (c - 1) % pieces not in turned:
                continue
            done.add(c)
            piece = jnp.where(lane < PC // 2, turned[(c - 1) % pieces], turned[c])
            span = slice(c * PC, (c + 1) * PC)
            out_ref[0, :, span] = piece.astype(BF16)
            slot = place_ref[visit * pieces + c]
            acc_ref[c % 2, slot] += inv_ref[visit, :, span] * piece

    for pair in range(min(pairs, pairs // GROUPS + 1)):
        fill(pair)
    for group in range(GROUPS):
        start, count = group * pairs // GROUPS, pairs // GROUPS
        main = blocks(start, count, cols_ref)
        for pair in range(start + count + 1, min(pairs, start + 2 * count + 1)):
            fill(pair)
        if group == GROUPS - 1:
            edge = blocks(pairs - 1, 1, edge_ref)[height:]
        for pair in range(start, start + count):
            for h in (0, 1):
                n = pair + h * pairs
                row = (2 * (pair - start) + h) * height
                block = main[row : row + height] if n < pieces - 1 else edge
                turned[n] = pltpu.roll(block, PC // 2, 1)
        finish()

    if last:
        @pl.when(step == pl.num_programs(0) - 1)
        def _():
            hand_out(order, acc_ref, keep_ref, send_ref)
            keep_ref[:, height:] = mine_ref[...] + other_ref[...]


def exchange(send, size, bit):
    return lax.ppermute(send, "tile", [(i, i ^ bit) for i in range(size)])


def on_device(image, inv_var, shift, col_offset, psf_rows, psf_cols, placement):
    visits, height, width = image.shape
    bases, length = psf_rows.shape[1:]
    size = lax.axis_size("tile")
    reach = length // 2 + TAPS
    if size & (size - 1) or reach != height - 1 or height % 8 or width % (8 * PC) or visits < 3:
        raise ValueError("unsupported sizes")
    index = lax.axis_index("tile").astype(jnp.int32)
    place = placement.reshape(-1) ^ index
    me = index.reshape(1)
    bits = [1 << b for b in range(size.bit_length() - 1)]
    order = [0]
    for bit in reversed(bits):
        order = order + [slot ^ bit for slot in order]
    order = tuple(order)
    near_pairs = [(i, i ^ 1) for i in range(size)]
    far_pairs = [(i, j) for j in range(size) for i in (j - 1 + 2 * (j % 2),) if 0 <= i < size]
    smem = pl.BlockSpec(memory_space=pltpu.SMEM)
    vmem = pl.BlockSpec(memory_space=pltpu.VMEM)
    anywhere = pl.BlockSpec(memory_space=pl.ANY)
    params = pltpu.CompilerParams(vmem_limit_bytes=GRANT)
    lanes = height * width // 8 - width // 8
    chunks = ((0, visits - 2), (visits - 2, 1), (visits - 1, 1))

    halos = []
    for (first, count) in chunks:
        block = pl.BlockSpec((1, 8, lanes), lambda v: (v, 0, 0))
        far, near = pl.pallas_call(
            pack_kernel,
            grid=(count,),
            in_specs=[smem, pl.BlockSpec((1, height, width), lambda v, first=first: (v + first, 0, 0))],
            out_specs=[block] * 2,
            out_shape=[jax.ShapeDtypeStruct((count, 8, lanes), F32)] * 2,
            compiler_params=params,
        )(me, image)
        far = lax.ppermute(far, "tile", far_pairs)
        near = lax.ppermute(near, "tile", near_pairs)
        halos.append((far, near))

    half = jax.ShapeDtypeStruct((size // 2, height, PC), F32)
    sums = pltpu.VMEM((2, size, height, PC), F32)
    weights = pl.pallas_call(
        functools.partial(weights_kernel, order),
        in_specs=[smem, vmem],
        out_specs=[vmem, vmem],
        out_shape=[half, half],
        scratch_shapes=[sums],
        compiler_params=params,
        name="weights",
    )
    den = weights(place, inv_var)
    denom = (den[0], exchange(den[1], size, bits[0]))

    deep = round_up(3 * round_up(3 * height, 16), 128)
    prepare = pl.pallas_call(
        functools.partial(prepare_kernel, height, size),
        in_specs=[smem, smem, smem, vmem, vmem],
        out_specs=[vmem] * 3,
        out_shape=[
            jax.ShapeDtypeStruct((visits, bases * height, deep), BF16),
            jax.ShapeDtypeStruct((visits, bases * WIDE, WIDE), BF16),
            jax.ShapeDtypeStruct((visits, bases * WIDE, WIDE), BF16),
        ],
        compiler_params=params,
        name="prepare",
    )
    operators = prepare(
        me, shift.T, col_offset, psf_rows.transpose(1, 0, 2), psf_cols.transpose(1, 0, 2)
    )

    carried = ()
    for (first, count), (far, near) in zip(chunks, halos):
        last = first + count == visits
        shapes = [jax.ShapeDtypeStruct((visits, height, width), BF16)]
        specs = [pl.BlockSpec((1, height, width), lambda v, first=first: (v + first, 0, 0))]
        pair_rows = (width // PC + 2) * height
        scratch = [pltpu.VMEM((bases, pair_rows, PC), BF16)] * 2
        inputs = [vmem] * 7
        extra = []
        if first:
            inputs += [vmem, anywhere]
            extra += [carried[1], carried[0]]
        if last:
            inputs += [vmem, vmem]
            extra += denom
            shapes += [jax.ShapeDtypeStruct((size // 2, 2 * height, PC), F32), half]
            specs += [vmem, vmem]
            scratch += [sums]
        else:
            shapes += [jax.ShapeDtypeStruct((2, size, height, PC), F32)]
            specs += [vmem]
        match = pl.pallas_call(
            functools.partial(match_kernel, bases, first, last, order),
            grid=(count,),
            in_specs=[smem] + inputs,
            out_specs=specs,
            out_shape=shapes,
            scratch_shapes=scratch,
            input_output_aliases={9: 0} if first else {},
            compiler_params=params,
            cost_estimate=pl.CostEstimate(
                flops=count * 6 * bases * height * width * WIDE,
                bytes_accessed=20 * count * height * width,
                transcendentals=0,
            ),
        )
        carried = match(place, far, near, image, inv_var, *operators, *extra)
    matched, keep, send = carried
    received = exchange(send, size, bits[0])
    keep = jnp.concatenate([keep[:, :height] + received, keep[:, height:]], axis=1)
    rest = bits[1:]
    while rest:
        near, rest = rest[:2], rest[2:]
        masks = [0, near[1], near[0], sum(near)] if len(near) > 1 else [0, near[0]]
        count = keep.shape[0] // len(masks)
        parts = {mask: keep[i * count : (i + 1) * count] for i, mask in enumerate(masks)}
        total = parts[0]
        for mask in sorted(parts, reverse=True)[:-1]:
            total = total + exchange(parts[mask], size, mask)
        keep = total
    return matched, keep[:, :height] / jnp.maximum(keep[:, height:], 1.0)


def solution(mesh):
    in_specs = (
        P(None, ("groups", "tile"), None),
        P(None, ("groups", "tile"), None),
        P("groups", None),
        P("groups"),
        P("groups", None, None),
        P("groups", None, None),
        P(("groups", "tile"), None),
    )
    out_specs = (P(None, ("groups", "tile"), None), P(("groups", "tile"), None, None))

    return jax.shard_map(
        on_device, mesh=mesh, in_specs=in_specs, out_specs=out_specs, check_vma=False
    )
```
